128 devices in a mesh: row: 8 (over y_lo, z), col: 16 (over x, y_hi, core).
Axes of the slice: x: 4, y: 4 (y_hi: 2, y_lo: 2; y = y_hi * 2 + y_lo), z: 4, core: 2. Of those that a mesh axis runs over, the one named last changes fastest.
Arguments:
- feats_one: bfloat16 [65536, 256], P(('row', 'col')), may hold values from -6 to 6
- feats_two: bfloat16 [65536, 256], P(('row', 'col')), may hold values from -6 to 6
- target_view: bfloat16 [65536, 256], P(('row', 'col')), may hold values from -6 to 6
- negatives: int32 [65536], P(('row', 'col')), may hold values from 0 to 511
- weight_one: bfloat16 [256, 256], replicated, may hold values from -0.375 to 0.375
- weight_two: bfloat16 [256, 256], replicated, may hold values from -0.375 to 0.375
- block_tiles: bfloat16 [81920, 128, 128], P(('row', 'col')), may hold values from -0.15625 to 0.15625
- tile_rows: int32 [81920], P(('row', 'col')), may hold values from 0 to 31
- tile_cols: int32 [81920], P(('row', 'col')), may hold values from 0 to 31
- block_counts: int32 [128], P(('row', 'col')), may hold values from 80 to 640, as said below
- need_rows: int32 [128, 16, 2], P(('row', 'col')), may hold values from 0 to 3, as said below
Outputs:
- grad_hidden: bfloat16 [65536, 256], P(('row', 'col'))
- grad_first: float32 [256, 256], replicated
- grad_second: float32 [256, 256], replicated
The draws below stay inside these ranges and needn't reach their ends.
Inputs may be any that keep to these rules, and one draw needn't show every extreme that they name: `need_rows`: for each owner and source, the 2 entries are distinct. `block_counts`: live tiles of one block list.
All inputs are finite; a program needn't handle non-finite values.
Results may differ from the reference program's by a relative error of at most 0.0063.
Values may be sent and summed in bfloat16 or wider, within the bound.
No kernel may reach another device: no remote copies, remote signals or barrier semaphores. Data moves between devices by JAX's collectives and lax.ppermute only.
A program may use at most 192 MiB of HBM per device.

```python
import math
import jax
import jax.numpy as jnp
from jax import lax

F = 256
TILE = 128
BLOCK_DEG = 160
NT_DEV = 4
NODE_DEV = 512
SLOT = 2
CAP = 640
SOURCES = 16
OWNERS = 128
ROW_SLOTS = 32
COL_TILES = 32
NODES = 65536
N_COL = 16


def draw_block_counts(key, part):
    lighter = jax.random.randint(jax.random.fold_in(key, 11), (OWNERS,), CAP // 8, CAP // 2 + 1)
    heaviest = jax.random.randint(jax.random.fold_in(key, 12), (), 0, OWNERS)
    return jnp.where(jnp.arange(OWNERS) == heaviest, CAP, lighter).astype(jnp.int32)


def draw_need_rows(key, part):
    subkeys = jax.random.split(jax.random.fold_in(key, 21), OWNERS * SOURCES)

    def one_list(subkey):
        return jax.random.permutation(subkey, NT_DEV)
    orders = jax.vmap(one_list)(subkeys)
    return orders[:, :SLOT].reshape(OWNERS, SOURCES, SLOT).astype(jnp.int32)


def plant(values, stream_key, least, largest):
    dims = values.shape
    index_at = [jax.random.randint(jax.random.fold_in(stream_key, axis), (), 0, dims[axis]) for axis in range(len(dims))]
    values = values.at[tuple(index_at)].set(least)
    longest = dims.index(max(dims))
    index_at[longest] = (index_at[longest] + 1) % dims[longest]
    return values.at[tuple(index_at)].set(largest)


def shard_levels(rng, extent, cuts, low, largest):
    def one(axis_at, parts):
        heights = jax.random.uniform(jax.random.fold_in(jax.random.fold_in(rng, 6), axis_at), (parts,), jnp.float32, low / len(cuts), largest / len(cuts))
        return jnp.repeat(jnp.exp(heights), extent[axis_at] // parts).reshape((-1,) + (1,) * (len(extent) - axis_at - 1))

    gain = one(*cuts[0])
    for cut in cuts[1:]:
        gain = gain * one(*cut)
    return gain


def noise(key, extent, width, most, cuts=(), kind=jnp.bfloat16):
    array = jax.random.normal(key, extent, jnp.float32) * width
    if len(cuts) > 0:
        array = shard_levels(key, extent, cuts, -0.22, 0.18) * array
    return jnp.clip(array, min=-most, max=most).astype(kind)


def setup_inputs(seed: int = 0) -> dict:
    key_list = jax.random.split(jax.random.key(seed), 12)
    return {
        "feats_one": noise(key_list[0], (NODES, F), 1.0, 6.0, ((0, 128),)),
        "feats_two": noise(key_list[1], (NODES, F), 1.0, 6.0, ((0, 128),)),
        "target_view": noise(key_list[2], (NODES, F), 1.0, 6.0, ((0, 128),)),
        "negatives": plant(jax.random.randint(key_list[3], (NODES,), 0, NODE_DEV), jax.random.fold_in(key_list[3], 1), 0, NODE_DEV - 1).astype(jnp.int32),
        "weight_one": noise(key_list[4], (F, F), F ** -0.5, 0.375),
        "weight_two": noise(key_list[5], (F, F), F ** -0.5, 0.375),
        "block_tiles": noise(key_list[6], (OWNERS * CAP, TILE, TILE), (TILE * BLOCK_DEG // 16) ** -0.5, 0.15625, ((0, 128),)),
        "tile_rows": plant(jax.random.randint(key_list[7], (OWNERS * CAP,), 0, ROW_SLOTS), jax.random.fold_in(key_list[7], 1), 0, ROW_SLOTS - 1).astype(jnp.int32),
        "tile_cols": plant(jax.random.randint(key_list[8], (OWNERS * CAP,), 0, COL_TILES), jax.random.fold_in(key_list[8], 1), 0, COL_TILES - 1).astype(jnp.int32),
        "block_counts": draw_block_counts(jax.random.fold_in(key_list[11], 71), 0),
        "need_rows": draw_need_rows(jax.random.fold_in(key_list[11], 71), 0),
    }


def silu_slope(values):
    sig = jax.nn.sigmoid(values)
    return sig * (1.0 + values * (1.0 - sig))

def reference(feats_one, feats_two, target_view, negatives, weight_one, weight_two, block_tiles, tile_rows, tile_cols, block_counts, need_rows):
    node_total = feats_two.shape[0]
    inverse_root = 1.0 / math.sqrt(F)
    pre_two = jnp.dot(feats_two, weight_two, preferred_element_type=jnp.float32)
    hidden = jax.nn.silu(pre_two)
    offsets = jnp.arange(node_total, dtype=jnp.int32) // NODE_DEV * NODE_DEV
    partner = offsets + negatives
    partner_rows = hidden[partner]
    target_full = target_view.astype(jnp.float32)
    s_pos = lax.optimization_barrier(jnp.sum(hidden * target_full, axis=-1)) * inverse_root
    s_neg = lax.optimization_barrier(jnp.sum(hidden * partner_rows, axis=-1)) * inverse_root
    prob_pos = jax.nn.sigmoid(-s_pos)
    prob_neg = jax.nn.sigmoid(s_neg)
    grad_out = -prob_pos[:, None] * target_full + prob_neg[:, None] * partner_rows
    grad_out = grad_out + jax.ops.segment_sum(prob_neg[:, None] * hidden, partner, num_segments=node_total)
    dpre_two = (grad_out * silu_slope(pre_two)).astype(jnp.bfloat16)
    grad_second = jnp.dot(feats_two.T, dpre_two, preferred_element_type=jnp.float32) * (1.0 / math.sqrt(NODES))
    message = jnp.dot(dpre_two, weight_two.T, preferred_element_type=jnp.float32).astype(jnp.bfloat16)
    entries = OWNERS * CAP
    entry_ids = jnp.arange(entries, dtype=jnp.int32)
    owner = entry_ids // CAP
    live = (entry_ids % CAP < block_counts[owner]).astype(jnp.float32)
    row_index = owner // N_COL
    col_index = owner % N_COL
    source = tile_rows // SLOT
    position = tile_rows % SLOT
    need_flat = need_rows.reshape(-1)
    local_tile = need_flat[(owner * SOURCES + source) * SLOT + position]
    row_tile = (row_index * N_COL + source) * NT_DEV + local_tile
    col_tile = (tile_cols // NT_DEV * N_COL + col_index) * NT_DEV + tile_cols % NT_DEV
    message_tiles = message.reshape(-1, TILE, F)
    block_len = 256 if entries % 256 == 0 else entries
    rounds = entries // block_len

    def add_block(summed_tiles, pieces):
        tile_part, row_part, col_part, live_part = pieces
        gathered = message_tiles[row_part].astype(jnp.float32)
        contrib = jnp.einsum('ktu,ktf->kuf', tile_part.astype(jnp.float32), gathered)
        contrib = contrib * live_part[:, None, None]
        return (summed_tiles + jax.ops.segment_sum(contrib, col_part, num_segments=node_total // TILE), None)
    start_tiles = jnp.zeros((node_total // TILE, TILE, F), jnp.float32)
    summed_tiles, _ = lax.scan(add_block, start_tiles, (block_tiles.reshape(rounds, block_len, TILE, TILE), row_tile.reshape(rounds, block_len), col_tile.reshape(rounds, block_len), live.reshape(rounds, block_len)))
    grad_hidden = summed_tiles.reshape(node_total, F).astype(jnp.bfloat16)
    pre_one = jnp.dot(feats_one, weight_one, preferred_element_type=jnp.float32)
    dpre_one = (grad_hidden.astype(jnp.float32) * silu_slope(pre_one)).astype(jnp.bfloat16)
    grad_first = jnp.dot(feats_one.T, dpre_one, preferred_element_type=jnp.float32) * (1.0 / math.sqrt(NODES))
    return (grad_hidden, grad_first, grad_second)
```

```python
import math

import jax
import jax.numpy as jnp
from jax import lax
from jax.experimental import pallas as pl
from jax.experimental.pallas import tpu as pltpu
from jax.sharding import PartitionSpec as P


BF16 = jnp.bfloat16
F32 = jnp.float32
TILE = 128
NODE_TILES = 4
SLOTS = 32
COLUMNS = 32
CHUNK = 64
UNROLL = 8
BATCH = 65536


def dot(left, right, left_dim, right_dim):
    return lax.dot_general(
        left, right, (((left_dim,), (right_dim,)), ((), ())), preferred_element_type=F32
    )


def silu_slope(values):
    sig = jax.nn.sigmoid(values)
    return sig, sig * (1.0 + values * (1.0 - sig))


def split_dot(selector, values):
    high = values.astype(BF16)
    low = (values - high.astype(F32)).astype(BF16)
    return dot(selector, high, 1, 0) + dot(selector, low, 1, 0)


def local_kernel(need, feats, target, neg_col, neg_row, weight, send, grad, message):
    nodes, features = feats.shape
    inverse_root = 1.0 / math.sqrt(features)
    pre = dot(feats[...], weight[...], 1, 0)
    sig, slope = silu_slope(pre)
    hidden = pre * sig
    lane = lax.broadcasted_iota(jnp.int32, (nodes, nodes), 1)
    sub = lax.broadcasted_iota(jnp.int32, (nodes, nodes), 0)
    pick = (neg_col[...] == lane).astype(F32).astype(BF16)
    spread = (neg_row[...] == sub).astype(F32).astype(BF16)
    partner = split_dot(pick, hidden)
    target_full = target[...].astype(F32)
    s_pos = jnp.sum(hidden * target_full, axis=1, keepdims=True) * inverse_root
    s_neg = jnp.sum(hidden * partner, axis=1, keepdims=True) * inverse_root
    prob_pos = jax.nn.sigmoid(-s_pos)
    prob_neg = jax.nn.sigmoid(s_neg)
    grad_out = prob_neg * partner - prob_pos * target_full
    grad_out = grad_out + split_dot(spread, prob_neg * hidden)
    dpre = (grad_out * slope).astype(BF16)
    grad[...] = dot(feats[...], dpre, 0, 0).astype(BF16)
    for tile in range(NODE_TILES):
        part = dpre[tile * TILE : (tile + 1) * TILE]
        message[tile] = dot(weight[...], part, 1, 1).astype(BF16)
    for slot in range(SLOTS):
        send[slot] = message[need[slot]]


def product_kernel(count, rows, cols, tiles, received, out, total):
    step = pl.program_id(0)
    live = count[0]

    @pl.when(step == 0)
    def _():
        total[...] = jnp.zeros_like(total)

    @pl.when(step * CHUNK < live)
    def _():
        def add(group, carry):
            for item in range(UNROLL):
                at = group * UNROLL + item
                tile = step * CHUNK + at
                col = jnp.where(tile < live, cols[tile], COLUMNS)
                total[col] += dot(received[rows[tile]], tiles[at], 1, 0)
            return carry

        lax.fori_loop(0, CHUNK // UNROLL, add, 0)

    @pl.when(step == pl.num_programs(0) - 1)
    def _():
        out[...] = total[pl.ds(0, COLUMNS)].astype(BF16)


def last_kernel(parts, feats, weight, hidden_grad, grad):
    pre = dot(feats[...], weight[...], 1, 0)
    _, slope = silu_slope(pre)
    rows = []
    for tile in range(NODE_TILES):
        total = parts[0, tile].astype(F32)
        for source in range(1, parts.shape[0]):
            total = total + parts[source, tile].astype(F32)
        rows.append(total.T.astype(BF16))
    value = jnp.concatenate(rows, axis=0)
    hidden_grad[...] = value
    dpre = (value.astype(F32) * slope).astype(BF16)
    grad[...] = dot(feats[...], dpre, 0, 0).astype(BF16)


def xor_permute(values, axes, size, mask):
    return lax.ppermute(values, axes, [(i, i ^ mask) for i in range(size)])


def sum_everywhere(part, scale):
    half = part.shape[0] // 2
    core = lax.axis_index("col") % 2
    kept = lax.dynamic_slice_in_dim(part, core * half, half, 0)
    sent = lax.dynamic_slice_in_dim(part, (1 - core) * half, half, 0)
    total = kept.astype(F32) + xor_permute(sent, "col", 16, 1).astype(F32)
    stages = (("col", 16, (4, 8, 12)), ("row", 8, (1, 2, 3)), (("row", "col"), 128, (64, 2, 66)))
    for axes, size, masks in stages:
        rounded = lax.optimization_barrier(total.astype(BF16))
        others = [xor_permute(rounded, axes, size, mask).astype(F32) for mask in masks]
        total = (rounded.astype(F32) + others[0]) + (others[1] + others[2])
    total = lax.optimization_barrier(total * scale)
    other = xor_permute(total, "col", 16, 1)
    first = jnp.where(core == 0, total, other)
    second = jnp.where(core == 0, other, total)
    return jnp.concatenate([first, second], axis=0)


def on_device(
    feats_one,
    feats_two,
    target_view,
    negatives,
    weight_one,
    weight_two,
    block_tiles,
    tile_rows,
    tile_cols,
    block_counts,
    need_rows,
):
    nodes, features = feats_two.shape
    capacity = block_tiles.shape[0]
    scale = 1.0 / math.sqrt(BATCH)
    vmem = pl.BlockSpec(memory_space=pltpu.VMEM)
    smem = pl.BlockSpec(memory_space=pltpu.SMEM)
    needed = lax.all_to_all(need_rows[0], "col", 0, 0).reshape(-1)
    slot_shape = (SLOTS, features, TILE)
    send, partial_second = pl.pallas_call(
        local_kernel,
        out_shape=(
            jax.ShapeDtypeStruct(slot_shape, BF16),
            jax.ShapeDtypeStruct((features, features), BF16),
        ),
        in_specs=[smem, vmem, vmem, vmem, vmem, vmem],
        out_specs=(vmem, vmem),
        scratch_shapes=[pltpu.VMEM((NODE_TILES, features, TILE), BF16)],
        compiler_params=pltpu.CompilerParams(vmem_limit_bytes=40 * 2**20),
        cost_estimate=pl.CostEstimate(
            flops=2 * 10 * nodes * nodes * features, bytes_accessed=2**22, transcendentals=2**18
        ),
    )(needed, feats_two, target_view, negatives[:, None], negatives[None, :], weight_two)
    received = lax.all_to_all(
        send.reshape(16, 2 * features, TILE), "col", 0, 0
    ).reshape(slot_shape)

    def tile_index(step, count, rows, cols):
        return (jnp.minimum(step, (count[0] + CHUNK - 1) // CHUNK - 1), 0, 0)

    sums = pl.pallas_call(
        product_kernel,
        out_shape=jax.ShapeDtypeStruct((COLUMNS, features, TILE), BF16),
        grid_spec=pltpu.PrefetchScalarGridSpec(
            num_scalar_prefetch=3,
            grid=(capacity // CHUNK,),
            in_specs=[
                pl.BlockSpec((CHUNK, TILE, TILE), tile_index),
                pl.BlockSpec(slot_shape, lambda step, *_: (0, 0, 0)),
            ],
            out_specs=pl.BlockSpec((COLUMNS, features, TILE), lambda step, *_: (0, 0, 0)),
            scratch_shapes=[pltpu.VMEM((COLUMNS + 1, features, TILE), F32)],
        ),
        compiler_params=pltpu.CompilerParams(vmem_limit_bytes=48 * 2**20),
        cost_estimate=pl.CostEstimate(
            flops=capacity * 2 * TILE * TILE * features,
            bytes_accessed=capacity * TILE * TILE * 2,
            transcendentals=0,
        ),
    )(block_counts, tile_rows, tile_cols, block_tiles, received)
    parts = lax.all_to_all(
        sums.reshape(8, NODE_TILES * features, TILE), "row", 0, 0
    ).reshape(8, NODE_TILES, features, TILE)
    grad_hidden, partial_first = pl.pallas_call(
        last_kernel,
        out_shape=(
            jax.ShapeDtypeStruct((nodes, features), BF16),
            jax.ShapeDtypeStruct((features, features), BF16),
        ),
        in_specs=[vmem, vmem, vmem],
        out_specs=(vmem, vmem),
        compiler_params=pltpu.CompilerParams(vmem_limit_bytes=40 * 2**20),
        cost_estimate=pl.CostEstimate(
            flops=2 * 2 * nodes * features * features,
            bytes_accessed=3 * 2**20,
            transcendentals=2**17,
        ),
    )(parts, feats_one, weight_one)
    return (
        grad_hidden,
        sum_everywhere(partial_first, scale),
        sum_everywhere(partial_second, scale),
    )


def solution(mesh):
    return jax.shard_map(
        on_device,
        mesh=mesh,
        in_specs=(
            P(("row", "col"), None),
            P(("row", "col"), None),
            P(("row", "col"), None),
            P(("row", "col")),
            P(),
            P(),
            P(("row", "col"), None, None),
            P(("row", "col")),
            P(("row", "col")),
            P(("row", "col")),
            P(("row", "col"), None, None),
        ),
        out_specs=(P(("row", "col"), None), P(), P()),
        check_vma=False,
    )
```
